32 devices in a mesh: grp: 4 (over x, core), mem: 8 (over z, y).
Axes of the slice: x: 2, y: 2, z: 4, core: 2. Of those that a mesh axis runs over, the one named last changes fastest.
Arguments:
- amplitudes: bfloat16 [384, 262144], P('mem', 'grp'), may hold values from -6 to 6
- integrals: bfloat16 [262144, 1024], P(('grp', 'mem')), may hold values from -0.0625 to 0.0625
- irrep_ef: int32 [262144], P(('grp', 'mem')), may hold values from 0 to 7
- irrep_ab: int32 [1024], replicated, may hold values from 0 to 7
Outputs:
- residual: float32 [384, 1024], P('mem', 'grp')
The draws below stay inside these ranges and needn't reach their ends.
All inputs are finite; a program needn't handle non-finite values.
Results may differ from the reference program's by a relative error of at most 0.0003.
Values may be sent and summed in bfloat16 or wider, within the bound.
No kernel may reach another device: no remote copies, remote signals or barrier semaphores. Data moves between devices by JAX's collectives and lax.ppermute only.
A program may use at most 128 MiB of HBM per device.

```python
import jax
import jax.numpy as jnp
from jax import lax

OP = 384
EF_DEV = 8192
AB = 1024
EF = 262144


def plant(result, key, smallest, largest):
    shape = result.shape
    place = [jax.random.randint(jax.random.fold_in(key, axis), (), 0, shape[axis]) for axis in range(len(shape))]
    result = result.at[tuple(place)].set(smallest)
    longest = shape.index(max(shape))
    place[longest] = (place[longest] + 1) % shape[longest]
    return result.at[tuple(place)].set(largest)


def raised(drawn, own_key, source, target, parts, factor):
    def block_of(dim):
        return (jnp.arange(drawn.shape[dim]) // (drawn.shape[dim] // parts)).reshape((-1,) + (1,) * (drawn.ndim - 1 - dim))

    near = jax.random.permutation(own_key, parts)[block_of(target)]
    other_side = (block_of(target) + parts // 2) % parts
    return jnp.where((block_of(source) == near) | (block_of(source) == other_side), factor * drawn, drawn)


def levels(stream_key, shape, shards, smallest, high):
    loudness, own = 1.0, jax.random.fold_in(stream_key, 6)
    for dim, shards_of in shards:
        draws = jnp.exp(jax.random.uniform(jax.random.fold_in(own, dim), (shards_of,), jnp.float32, smallest / len(shards), high / len(shards)))
        loudness = loudness * jnp.repeat(draws, shape[dim] // shards_of).reshape([-1 if axis == dim else 1 for axis in range(len(shape))])
    return loudness


def noise(own_key, dims, width, bound, split=(), held_as=jnp.bfloat16):
    gain = levels(own_key, dims, split, -0.22, 0.18) if split else 1.0
    entries = jax.random.normal(own_key, dims, jnp.float32) * width * gain
    return jnp.minimum(jnp.maximum(entries, -bound), bound).astype(held_as)


def gaussian_with(own_key, extent, width, most, pieces, heavy, kind=jnp.bfloat16):
    drawn = width * jax.random.normal(own_key, extent, jnp.float32)
    if pieces:
        drawn = drawn * levels(own_key, extent, pieces, -0.22, 0.18)
    return jnp.clip(raised(drawn, jax.random.fold_in(own_key, 3), *heavy), -most, most).astype(kind)


def setup_inputs(seed: int = 0) -> dict:
    streams_of = jax.random.split(jax.random.key(seed), 5)
    amplitudes = noise(streams_of[0], (OP, EF), 1.0, 6.0, ((0, 8), (1, 4)))
    integrals = gaussian_with(streams_of[1], (EF, AB), (EF // 8) ** -0.5, 0.0625, ((0, 32),), (0, 1, 32, 2.75))
    irrep_ef = plant(jax.random.randint(streams_of[2], (EF,), 0, 8), jax.random.fold_in(streams_of[2], 1), 0, 7).astype(jnp.int32)
    irrep_ab = plant(jax.random.randint(streams_of[3], (AB,), 0, 8), jax.random.fold_in(streams_of[3], 1), 0, 7).astype(jnp.int32)
    return dict(amplitudes=amplitudes, integrals=integrals, irrep_ef=irrep_ef, irrep_ab=irrep_ab)


def reference(amplitudes, integrals, irrep_ef, irrep_ab):
    def add_block(index, total):
        start = (index * EF_DEV).astype(jnp.int32)
        left = lax.dynamic_slice_in_dim(amplitudes, start, EF_DEV, 1)
        right = lax.dynamic_slice_in_dim(integrals, start, EF_DEV, 0)
        labels = lax.dynamic_slice_in_dim(irrep_ef, start, EF_DEV, 0)
        allowed = labels[:, None] == irrep_ab[None, :]
        blocked = jnp.where(allowed, right, jnp.zeros_like(right))
        return total + jnp.dot(left, blocked, preferred_element_type=jnp.float32)

    empty = jnp.zeros((OP, AB), jnp.float32)
    return lax.fori_loop(0, EF // EF_DEV, add_block, empty)
```

```python
import jax
import jax.numpy as jnp
from jax import lax
from jax.sharding import PartitionSpec as P


def swap(value, axis, distance):
    count = lax.axis_size(axis)
    return lax.ppermute(value, axis, [(i, i ^ distance) for i in range(count)])


def reversed_bits(count):
    levels = count.bit_length() - 1
    return [sum(((p >> i) & 1) << (levels - 1 - i) for i in range(levels)) for p in range(count)]


def issue_order(members):
    half = members // 2
    return [d for j in range(half) for d in (members - 1 - j, half - 1 - j) if d]


def row_chunks(rows):
    if rows % 48:
        return [rows]
    unit = rows // 6
    return [3 * unit, 2 * unit, unit]


def local(amplitudes, integrals, irrep_ef, irrep_ab):
    members = lax.axis_size("mem")
    groups = lax.axis_size("grp")
    me = lax.axis_index("mem")
    group = lax.axis_index("grp")
    pairs = integrals.shape[0]
    width = integrals.shape[1] // groups
    allowed = irrep_ef[:, None] == irrep_ab[None, :]
    blocked = jnp.where(allowed, integrals, jnp.zeros_like(integrals))

    sizes = row_chunks(amplitudes.shape[0])
    starts = [sum(sizes[:i]) for i in range(len(sizes))]
    order = reversed_bits(members)
    arrived = []
    for first, size in zip(starts, sizes):
        got = {}
        for distance in issue_order(members) + [0]:
            column = (me ^ distance) * pairs
            piece = lax.dynamic_slice(amplitudes, (first, column), (size, pairs))
            got[distance] = swap(piece, "mem", distance) if distance else piece
        arrived.append(jnp.concatenate([got[d] for d in order], 0))

    shares = []
    for left in arrived:
        value = jnp.dot(left, blocked, preferred_element_type=jnp.float32)
        tall = value.shape[0]
        blocks = [
            lax.dynamic_slice_in_dim(value, (group ^ j) * width, width, 1)
            for j in range(groups)
        ]
        bit = 1
        while bit < groups:
            sent = jnp.concatenate(blocks[1::2], 0)
            kept = jnp.concatenate(blocks[0::2], 0)
            came = swap(sent, "grp", bit)
            kept = kept + came
            blocks = [kept[i * tall:(i + 1) * tall] for i in range(len(blocks) // 2)]
            bit *= 2
        share = blocks[0]
        bit = 1
        while bit < members:
            half = share.shape[0] // 2
            came = swap(share[half:], "mem", bit)
            share = share[:half] + came
            bit *= 2
        shares.append(share)
    return jnp.concatenate(shares, 0)


def solution(mesh):
    placed = (P("mem", "grp"), P(("grp", "mem"), None), P(("grp", "mem")), P())
    return jax.shard_map(
        local, mesh=mesh, in_specs=placed, out_specs=P("mem", "grp"), check_vma=False
    )
```

```python
import jax
import jax.numpy as jnp
from jax import lax
from jax.experimental import pallas as pl
from jax.experimental.pallas import tpu as pltpu
from jax.sharding import PartitionSpec as P

SHARES = (1, 2, 3)
LANES = 128


def swap(value, axis, distance):
    count = lax.axis_size(axis)
    return lax.ppermute(value, axis, [(i, i ^ distance) for i in range(count)])


def reversed_bits(count):
    levels = count.bit_length() - 1
    return [sum(((p >> i) & 1) << (levels - 1 - i) for i in range(levels)) for p in range(count)]


def row_chunks(rows):
    if rows % (8 * sum(SHARES)):
        return [rows]
    unit = rows // sum(SHARES)
    return [share * unit for share in SHARES]


def blocked_dot_kernel(group, *refs):
    pieces, (values, labels, targets, kept, sent, total) = refs[:-6], refs[-6:]
    left = jnp.concatenate([piece[...] for piece in pieces], 0)
    label = labels[...]
    columns = []
    for j in range(values.shape[1] // LANES):
        at = slice(j * LANES, (j + 1) * LANES)
        part = values[:, at]
        columns.append(jnp.where(label == targets[:, at], part, jnp.zeros_like(part)))
    term = jnp.dot(left, jnp.concatenate(columns, 1), preferred_element_type=jnp.float32)
    step = pl.program_id(0)

    @pl.when(step == 0)
    def _():
        total[...] = term

    @pl.when(step > 0)
    def _():
        total[...] += term

    @pl.when(step == pl.num_programs(0) - 1)
    def _():
        rows, width = total.shape[0], kept.shape[1]
        groups = total.shape[1] // width
        for j in range(groups):
            start = pl.multiple_of((group[0] ^ j) * width, LANES)
            out = sent if j % 2 else kept
            out[(j // 2) * rows:(j // 2 + 1) * rows, :] = total[:, pl.ds(start, width)]


def blocked_dot(pieces, values, labels, targets, group, groups):
    pairs, columns = values.shape
    rows = sum(piece.shape[0] for piece in pieces)
    slab = next(s for s in (2048, 1024, 512, 256, 128, pairs) if pairs % s == 0)
    width = columns // groups
    half = jax.ShapeDtypeStruct((rows * groups // 2, width), jnp.float32)
    spec = pltpu.PrefetchScalarGridSpec(
        num_scalar_prefetch=1,
        grid=(pairs // slab,),
        in_specs=[pl.BlockSpec((piece.shape[0], slab), lambda k, g: (0, k)) for piece in pieces]
        + [
            pl.BlockSpec((slab, columns), lambda k, g: (k, 0)),
            pl.BlockSpec((slab, LANES), lambda k, g: (k, 0)),
            pl.BlockSpec((1, columns), lambda k, g: (0, 0)),
        ],
        out_specs=[pl.BlockSpec(half.shape, lambda k, g: (0, 0))] * 2,
        scratch_shapes=[pltpu.VMEM((rows, columns), jnp.float32)],
    )
    return pl.pallas_call(
        blocked_dot_kernel,
        grid_spec=spec,
        out_shape=[half, half],
        cost_estimate=pl.CostEstimate(
            flops=2 * rows * pairs * columns, bytes_accessed=2 * pairs * columns, transcendentals=0
        ),
        compiler_params=pltpu.CompilerParams(vmem_limit_bytes=16 << 20),
    )(group, *pieces, values, labels, targets)


def columns_to_owner(pieces, blocked, groups):
    kept, sent = blocked(pieces)
    bit = 1
    while bit < groups:
        came = swap(sent, "grp", bit)
        kept = kept + came
        bit *= 2
        if bit < groups:
            tall = kept.shape[0] * bit // groups
            blocks = [kept[i * tall:(i + 1) * tall] for i in range(groups // bit)]
            kept, sent = jnp.concatenate(blocks[0::2], 0), jnp.concatenate(blocks[1::2], 0)
    return kept


def fold(shares, distance):
    halves = [share.shape[0] // 2 for share in shares]
    out = jnp.concatenate([share[h:] for share, h in zip(shares, halves)], 0)
    came = swap(out, "mem", distance)
    kept = jnp.concatenate([share[:h] for share, h in zip(shares, halves)], 0) + came
    return cut(kept, halves)


def cut(value, sizes):
    ends = [sum(sizes[:i]) for i in range(len(sizes) + 1)]
    return [value[i:j] for i, j in zip(ends, ends[1:])]


def local(amplitudes, integrals, irrep_ef, irrep_ab):
    members = lax.axis_size("mem")
    groups = lax.axis_size("grp")
    me = lax.axis_index("mem")
    group = jnp.reshape(lax.axis_index("grp"), (1,)).astype(jnp.int32)
    rows, pairs = amplitudes.shape[0], integrals.shape[0]
    half, quarter = members // 2, members // 4
    labels = jnp.broadcast_to(irrep_ef.astype(jnp.bfloat16)[:, None], (pairs, LANES))
    targets = irrep_ab.astype(jnp.bfloat16)[None, :]

    def blocked(pieces):
        if any(piece.shape[0] % 8 for piece in pieces):
            pieces = [jnp.concatenate(pieces, 0)]
        return blocked_dot(pieces, integrals, labels, targets, group, groups)

    sizes = row_chunks(rows)
    far_ranges = [(sum(sizes[:c]), size) for c, size in enumerate(sizes)]
    near_ranges = [(0, sizes[0])] + [(sizes[0], rows - sizes[0])] * (len(sizes) > 1)
    source = amplitudes

    def piece(span, distance):
        return lax.dynamic_slice(source, (span[0], (me ^ distance) * pairs), (span[1], pairs))

    lead = piece(far_ranges[0], members - 1)
    source, lead = lax.optimization_barrier((source, lead))
    far, near = [], []
    for c, span in enumerate(far_ranges):
        outs = {d: lead if c == 0 and d == members - 1 else piece(span, d) for d in range(half, members)}
        far.append({d: swap(out, "mem", d) for d, out in outs.items()})
    for span in near_ranges:
        outs = {d: piece(span, d) for d in range(half)}
        near.append({d: swap(out, "mem", d) if d else out for d, out in outs.items()})

    order = reversed_bits(half)
    far_shares, near_shares = [], []
    for c, got in enumerate(near):
        parts = [[got[d] for d in order]]
        if c < len(far) - 1:
            parts.append([far[c][half + d] for d in order])
        kept = columns_to_owner(sum(parts, []), blocked, groups)
        shares = cut(kept, [sum(p.shape[0] for p in part) for part in parts])
        if half > 1:
            shares = fold(shares, 1)
        near_shares.append(shares[0])
        far_shares += shares[1:]
    bit = 2
    while bit < half:
        shares = fold(near_shares + far_shares, bit)
        near_shares, far_shares = shares[:len(near_shares)], shares[len(near_shares):]
        bit *= 2
    across = []
    if far_shares:
        across.append(swap(jnp.concatenate(far_shares, 0), "mem", half))
    total = None
    for low in (half + quarter, half):
        ends = [far[-1][low + d] for d in range(quarter)]
        share = columns_to_owner(ends, blocked, groups)
        for d, block in reversed(list(enumerate(cut(share, [sizes[-1]] * quarter)))):
            came = swap(block, "mem", low + d)
            total = came if total is None else total + came
    return jnp.concatenate(near_shares, 0) + jnp.concatenate(across + [total], 0)


def solution(mesh):
    placed = (P("mem", "grp"), P(("grp", "mem"), None), P(("grp", "mem")), P())
    return jax.shard_map(
        local, mesh=mesh, in_specs=placed, out_specs=P("mem", "grp"), check_vma=False
    )
```

```python
import functools

import jax
import jax.numpy as jnp
from jax import lax
from jax.experimental import pallas as pl
from jax.experimental.pallas import tpu as pltpu
from jax.sharding import PartitionSpec as P

SHARES = (1, 2, 3)
LANES = 128


def swap(value, axis, distance):
    count = lax.axis_size(axis)
    return lax.ppermute(value, axis, [(i, i ^ distance) for i in range(count)])


def reversed_bits(count):
    levels = count.bit_length() - 1
    return [sum(((p >> i) & 1) << (levels - 1 - i) for i in range(levels)) for p in range(count)]


def row_chunks(rows):
    if rows % (8 * sum(SHARES)):
        return [rows]
    unit = rows // sum(SHARES)
    return [share * unit for share in SHARES]


def product_kernel(blocks, group, *refs):
    pieces, values, out = refs[:-2], refs[-2], refs[-1]
    rows, width = out.shape[0] // len(blocks), out.shape[1]
    pairs = values.shape[0]
    slab = next(s for s in (1024, 512, 256, 128, pairs) if pairs % s == 0)
    for k in range(pairs // slab):
        at = slice(k * slab, (k + 1) * slab)
        left = jnp.concatenate([piece[:, at] for piece in pieces], 0)
        for i, j in enumerate(blocks):
            start = pl.multiple_of((group[0] ^ j) * width, LANES)
            right = values[at, pl.ds(start, width)]
            term = jnp.dot(left, right, preferred_element_type=jnp.float32)
            rest = slice(i * rows, (i + 1) * rows)
            out[rest, :] = term if k == 0 else out[rest, :] + term


def product(pieces, values, group, groups, blocks):
    pairs, columns = values.shape
    rows = sum(piece.shape[0] for piece in pieces)
    out = jax.ShapeDtypeStruct((rows * len(blocks), columns // groups), jnp.float32)
    whole = pl.BlockSpec(memory_space=pltpu.VMEM)
    return pl.pallas_call(
        functools.partial(product_kernel, blocks),
        in_specs=[pl.BlockSpec(memory_space=pltpu.SMEM)] + [whole] * (len(pieces) + 1),
        out_specs=whole,
        out_shape=out,
        cost_estimate=pl.CostEstimate(
            flops=2 * pairs * out.shape[0] * out.shape[1],
            bytes_accessed=2 * pairs * columns * len(blocks) // groups,
            transcendentals=0,
        ),
        compiler_params=pltpu.CompilerParams(vmem_limit_bytes=12 << 20),
    )(group, *pieces, values)


def columns_to_owner(pieces, product_of, groups):
    rows = sum(piece.shape[0] for piece in pieces)
    came = {j: [] for j in range(groups)}

    def term(blocks):
        return product_of(pieces, blocks)

    bit = 1
    while bit < groups:
        blocks = range(bit, groups, 2 * bit)
        out = term(blocks)
        if came[bit]:
            out = out + sum(jnp.concatenate(parts, 0) for parts in zip(*[came[j] for j in blocks]))
        got = cut(swap(out, "grp", bit), [rows] * len(blocks))
        for j, part in zip(blocks, got):
            came[j - bit].append(part)
        bit *= 2
    out = term([0])
    return out + sum(came[0])


def fold(shares, distance):
    halves = [share.shape[0] // 2 for share in shares]
    out = jnp.concatenate([share[h:] for share, h in zip(shares, halves)], 0)
    came = swap(out, "mem", distance)
    kept = jnp.concatenate([share[:h] for share, h in zip(shares, halves)], 0) + came
    return cut(kept, halves)


def cut(value, sizes):
    ends = [sum(sizes[:i]) for i in range(len(sizes) + 1)]
    return [value[i:j] for i, j in zip(ends, ends[1:])]


def local(amplitudes, integrals, irrep_ef, irrep_ab):
    members = lax.axis_size("mem")
    groups = lax.axis_size("grp")
    me = lax.axis_index("mem")
    group = jnp.reshape(lax.axis_index("grp"), (1,)).astype(jnp.int32)
    rows, pairs = amplitudes.shape[0], integrals.shape[0]
    half, quarter = members // 2, members // 4
    allowed = irrep_ef[:, None] == irrep_ab[None, :]
    values = jnp.where(allowed, integrals, jnp.zeros_like(integrals))
    values = pltpu.with_memory_space_constraint(values, pltpu.VMEM)

    def blocked(pieces, blocks):
        if any(piece.shape[0] % 8 for piece in pieces):
            pieces = [jnp.concatenate(pieces, 0)]
        return product(pieces, values, group, groups, tuple(blocks))

    sizes = row_chunks(rows)
    far_ranges = [(sum(sizes[:c]), size) for c, size in enumerate(sizes)]
    source = amplitudes

    def piece(span, distance):
        return lax.dynamic_slice(source, (span[0], (me ^ distance) * pairs), (span[1], pairs))

    leads = [members - 1, members - 2]
    source, *leading = lax.optimization_barrier((source, *[piece(far_ranges[0], d) for d in leads]))
    leading = dict(zip(leads, leading))
    far = []
    for c, span in enumerate(far_ranges):
        outs = {d: piece(span, d) for d in range(half, members)}
        if c == 0:
            outs.update(leading)
        far.append({d: swap(out, "mem", d) for d, out in outs.items()})
    near = {d: piece((0, rows), d) for d in range(half)}
    near = {d: swap(out, "mem", d) if d else out for d, out in near.items()}

    order = reversed_bits(half)
    batches = [[[got[half + d] for d in order]] for got in far[:-1]] or [[]]
    batches[-1].append([near[d] for d in order])
    every = []
    for parts in batches:
        kept = columns_to_owner(sum(parts, []), blocked, groups)
        shares = cut(kept, [sum(p.shape[0] for p in part) for part in parts])
        if half > 1:
            shares = fold(shares, 1)
        every += shares
    bit = 2
    while bit < half:
        every = fold(every, bit)
        bit *= 2
    far_shares, near_share = every[:-1], every[-1]
    across = []
    if far_shares:
        across.append(swap(jnp.concatenate(far_shares, 0), "mem", half))
    folded = reversed_bits(quarter)
    ends = [far[-1][half + quarter + d] for d in folded]
    share = columns_to_owner(ends, blocked, groups)
    bit = 1
    while bit < quarter:
        [share] = fold([share], bit)
        bit *= 2
    joined = swap(share, "mem", quarter)
    share = columns_to_owner([far[-1][half + d] for d in range(quarter)], blocked, groups)
    blocks = cut(share, [sizes[-1]] * quarter)
    blocks[0] = blocks[0] + joined
    total = None
    for d in range(quarter - 1, -1, -1):
        came = swap(blocks[d], "mem", half + d)
        total = came if total is None else total + came
    return near_share + jnp.concatenate(across + [total], 0)


def solution(mesh):
    placed = (P("mem", "grp"), P(("grp", "mem"), None), P(("grp", "mem")), P())
    return jax.shard_map(
        local, mesh=mesh, in_specs=placed, out_specs=P("mem", "grp"), check_vma=False
    )
```

```python
import functools

import jax
import jax.numpy as jnp
from jax import lax
from jax.experimental import pallas as pl
from jax.experimental.pallas import tpu as pltpu
from jax.sharding import PartitionSpec as P

SHARES = (1, 2, 3)
LANES = 128


def swap(value, axis, distance):
    count = lax.axis_size(axis)
    return lax.ppermute(value, axis, [(i, i ^ distance) for i in range(count)])


def reversed_bits(count):
    levels = count.bit_length() - 1
    return [sum(((p >> i) & 1) << (levels - 1 - i) for i in range(levels)) for p in range(count)]


def row_chunks(rows):
    if rows % (8 * sum(SHARES)):
        return [rows]
    unit = rows // sum(SHARES)
    return [share * unit for share in SHARES]


def product_kernel(blocks, group, *refs):
    pieces, values, out = refs[:-2], refs[-2], refs[-1]
    rows, width = out.shape[0] // len(blocks), out.shape[1]
    pairs = values.shape[0]
    slab = next(s for s in (1024, 512, 256, 128, pairs) if pairs % s == 0)
    for k in range(pairs // slab):
        at = slice(k * slab, (k + 1) * slab)
        left = jnp.concatenate([piece[:, at] for piece in pieces], 0)
        for i, j in enumerate(blocks):
            start = pl.multiple_of((group[0] ^ j) * width, LANES)
            right = values[at, pl.ds(start, width)]
            term = jnp.dot(left, right, preferred_element_type=jnp.float32)
            rest = slice(i * rows, (i + 1) * rows)
            out[rest, :] = term if k == 0 else out[rest, :] + term


def product(pieces, values, group, groups, blocks):
    pairs, columns = values.shape
    rows = sum(piece.shape[0] for piece in pieces)
    out = jax.ShapeDtypeStruct((rows * len(blocks), columns // groups), jnp.float32)
    whole = pl.BlockSpec(memory_space=pltpu.VMEM)
    return pl.pallas_call(
        functools.partial(product_kernel, blocks),
        in_specs=[pl.BlockSpec(memory_space=pltpu.SMEM)] + [whole] * (len(pieces) + 1),
        out_specs=whole,
        out_shape=out,
        cost_estimate=pl.CostEstimate(
            flops=2 * pairs * out.shape[0] * out.shape[1],
            bytes_accessed=2 * pairs * columns * len(blocks) // groups,
            transcendentals=0,
        ),
        compiler_params=pltpu.CompilerParams(vmem_limit_bytes=12 << 20),
    )(group, *pieces, values)


def columns_to_owner(pieces, product_of, groups):
    def total(j, count):
        if count == 1:
            return product_of(pieces, [j])
        bit = count // 2
        came = swap(total(j + bit, bit), "grp", bit)
        own = total(j, bit)
        return own + came

    return total(0, groups)


def fold(shares, distance):
    halves = [share.shape[0] // 2 for share in shares]
    out = jnp.concatenate([share[h:] for share, h in zip(shares, halves)], 0)
    came = swap(out, "mem", distance)
    kept = jnp.concatenate([share[:h] for share, h in zip(shares, halves)], 0) + came
    return cut(kept, halves)


def cut(value, sizes):
    ends = [sum(sizes[:i]) for i in range(len(sizes) + 1)]
    return [value[i:j] for i, j in zip(ends, ends[1:])]


def local(amplitudes, integrals, irrep_ef, irrep_ab):
    members = lax.axis_size("mem")
    groups = lax.axis_size("grp")
    me = lax.axis_index("mem")
    group = jnp.reshape(lax.axis_index("grp"), (1,)).astype(jnp.int32)
    rows, pairs = amplitudes.shape[0], integrals.shape[0]
    half, quarter = members // 2, members // 4
    allowed = irrep_ef[:, None] == irrep_ab[None, :]
    values = jnp.where(allowed, integrals, jnp.zeros_like(integrals))
    values = pltpu.with_memory_space_constraint(values, pltpu.VMEM)

    def blocked(pieces, blocks):
        if any(piece.shape[0] % 8 for piece in pieces):
            pieces = [jnp.concatenate(pieces, 0)]
        return product(pieces, values, group, groups, tuple(blocks))

    sizes = row_chunks(rows)
    far_ranges = [(sum(sizes[:c]), size) for c, size in enumerate(sizes)]
    source = amplitudes

    def piece(span, distance):
        return lax.dynamic_slice(source, (span[0], (me ^ distance) * pairs), (span[1], pairs))

    leads = [members - 1, members - 2]
    source, *leading = lax.optimization_barrier((source, *[piece(far_ranges[0], d) for d in leads]))
    leading = dict(zip(leads, leading))
    far = []
    for c, span in enumerate(far_ranges):
        outs = {d: piece(span, d) for d in range(half, members)}
        if c == 0:
            outs.update(leading)
        far.append({d: swap(out, "mem", d) for d, out in outs.items()})
    near = {d: piece((0, rows), d) for d in range(half)}
    near = {d: swap(out, "mem", d) if d else out for d, out in near.items()}

    order = reversed_bits(half)
    batches = [[[got[half + d] for d in order]] for got in far[:-1]] or [[]]
    batches[-1].append([near[d] for d in order])
    every = []
    for parts in batches:
        kept = columns_to_owner(sum(parts, []), blocked, groups)
        shares = cut(kept, [sum(p.shape[0] for p in part) for part in parts])
        if half > 1:
            shares = fold(shares, 1)
        every += shares
    bit = 2
    while bit < half:
        every = fold(every, bit)
        bit *= 2
    far_shares, near_share = every[:-1], every[-1]
    across = []
    if far_shares:
        across.append(swap(jnp.concatenate(far_shares, 0), "mem", half))
    folded = reversed_bits(quarter)
    ends = [far[-1][half + quarter + d] for d in folded]
    share = columns_to_owner(ends, blocked, groups)
    bit = 1
    while bit < quarter:
        [share] = fold([share], bit)
        bit *= 2
    joined = swap(share, "mem", quarter)
    share = columns_to_owner([far[-1][half + d] for d in range(quarter)], blocked, groups)
    blocks = cut(share, [sizes[-1]] * quarter)
    blocks[0] = blocks[0] + joined
    total = None
    for d in range(quarter):
        came = swap(blocks[d], "mem", half + d)
        total = came if total is None else total + came
    return near_share + jnp.concatenate(across + [total], 0)


def solution(mesh):
    placed = (P("mem", "grp"), P(("grp", "mem"), None), P(("grp", "mem")), P())
    return jax.shard_map(
        local, mesh=mesh, in_specs=placed, out_specs=P("mem", "grp"), check_vma=False
    )
```
